512 devices in a mesh: off: 8 (over x, core), inl: 16 (over y_hi, z), xl: 4 (over y_lo).
Axes of the slice: x: 4, y: 8 (y_hi: 2, y_lo: 4; y = y_hi * 4 + y_lo), z: 8, core: 2. Of those that a mesh axis runs over, the one named last changes fastest.
Arguments:
- gathers: bfloat16 [32, 128, 64, 256], P('off', 'inl', 'xl'), may hold values from -108 to 108
- shift_start: float32 [32, 128, 64, 256], P('off', 'inl', 'xl'), may hold values from -1.5 to 1.5
Outputs:
- shifts: float32 [32, 128, 64, 256], P('off', 'inl', 'xl')
The draws below stay inside these ranges and needn't reach their ends.
All inputs are finite; a program needn't handle non-finite values.
Results may differ from the reference program's by a relative error of at most 0.002.
Values may be sent and summed in bfloat16 or wider, within the bound.
No kernel may reach another device: no remote copies, remote signals or barrier semaphores. Data moves between devices by JAX's collectives and lax.ppermute only.
A program may use at most 64 MiB of HBM per device.

```python
import jax
import jax.numpy as jnp
from jax import lax

NT = 256
ITERS = 3
OFFSETS = 32
IL = 128
XL = 64


def draw_gathers(key, part):
    common_key = jax.random.fold_in(key, 11)
    noise_key = jax.random.fold_in(key, 12)
    common = jnp.clip(jax.random.normal(common_key, (IL, XL, NT), jnp.float32), -6.0, 6.0)
    noise_part = jnp.clip(jax.random.normal(noise_key, (OFFSETS, IL, XL, NT), jnp.float32), -6.0, 6.0)
    traces = common[None] + 0.8 * noise_part
    return traces.astype(jnp.bfloat16)


def shard_levels(stream_key, dims, shards, smallest, high):
    loudness, own = 1.0, jax.random.fold_in(stream_key, 6)
    for dim, blocks in shards:
        heights = jnp.exp(jax.random.uniform(jax.random.fold_in(own, dim), (blocks,), jnp.float32, smallest / len(shards), high / len(shards)))
        loudness = loudness * jnp.repeat(heights, dims[dim] // blocks).reshape([-1 if axis == dim else 1 for axis in range(len(dims))])
    return loudness


def setup_inputs(seed: int = 0) -> dict:
    key_list = jax.random.split(jax.random.key(seed), 3)
    return {
        "gathers": draw_gathers(jax.random.fold_in(key_list[2], 71), 0),
        "shift_start": jnp.clip(jax.random.uniform(key_list[1], (OFFSETS, IL, XL, NT), jnp.float32, -1.5, 1.5) * shard_levels(key_list[1], (OFFSETS, IL, XL, NT), ((0, 8), (1, 16), (2, 4)), -0.4, 0.0), -1.5, 1.5),
    }


tap_reach = 5
max_lag = 4
ramp_width = 40.0
score_gain = 4.0
shift_limit = 2.0
eps = 1e-05
binomial = (0.0625, 0.25, 0.375, 0.25, 0.0625)

def taper_weight(offset_value):
    inside = jnp.abs(offset_value) < 6.0
    window = jnp.square(jnp.cos(jnp.pi * offset_value / 12.0))
    return jnp.where(inside, jnp.sinc(offset_value) * window, 0.0)

def warp_traces(traces, shifts):
    length = traces.shape[-1]
    last_axis = traces.ndim - 1
    pad_widths = [(0, 0)] * last_axis + [(tap_reach, tap_reach)]
    padded = jnp.pad(traces, pad_widths)
    summed = jnp.zeros(shifts.shape, jnp.float32)
    for tap_index in range(-tap_reach, tap_reach + 1):
        segment = lax.slice_in_dim(padded, tap_reach + tap_index, tap_reach + tap_index + length, axis=last_axis)
        summed = summed + taper_weight(tap_index - shifts) * segment.astype(jnp.float32)
    return summed

def lagged_copy(values, lag_value):
    length = values.shape[-1]
    last_axis = values.ndim - 1
    pad_widths = [(0, 0)] * last_axis + [(max_lag, max_lag)]
    padded = jnp.pad(values, pad_widths)
    return lax.slice_in_dim(padded, max_lag + lag_value, max_lag + lag_value + length, axis=last_axis)

def ramp_matrix(length):
    positions = jnp.arange(length)
    spacing = jnp.abs(positions[:, None] - positions[None, :]).astype(jnp.float32)
    return (jnp.maximum(ramp_width - spacing, 0.0) / ramp_width).astype(jnp.bfloat16)

def blur_axis(padded, axis_index, length):
    summed = jnp.zeros((), jnp.float32)
    for offset_index, weight_value in enumerate(binomial):
        summed = summed + weight_value * lax.slice_in_dim(padded, offset_index, offset_index + length, axis=axis_index)
    return summed

def lateral_blur(field, axis_first, axis_second):
    pad_widths = [(0, 0)] * field.ndim
    pad_widths[axis_first] = (2, 2)
    pad_widths[axis_second] = (2, 2)
    padded = jnp.pad(field, pad_widths)
    along_first = blur_axis(padded, axis_first, field.shape[axis_first])
    return blur_axis(along_first, axis_second, field.shape[axis_second])

def wide_rows(rows, smoother):
    return jnp.dot(rows.astype(jnp.float32), smoother.astype(jnp.float32), preferred_element_type=jnp.float32)

def shift_update(warped, pilot_trace, pilot_energy, smoother, smooth_rows):
    pilot_wide = pilot_trace.astype(jnp.float32)
    products = []
    energies = []
    for lag_value in range(-max_lag, max_lag + 1):
        lagged = lagged_copy(warped, lag_value).astype(jnp.float32)
        products.append((pilot_wide * lagged).astype(jnp.bfloat16))
        energies.append(jnp.square(lagged).astype(jnp.bfloat16))
    stacked = jnp.stack(products + energies)
    smoothed = smooth_rows(stacked.reshape(-1, stacked.shape[-1]), smoother).reshape(stacked.shape)
    lag_total = 2 * max_lag + 1
    coherence = smoothed[:lag_total] / jnp.sqrt(pilot_energy[None] * smoothed[lag_total:] + eps)
    scores = jnp.exp(score_gain * coherence)
    lag_values = jnp.arange(-max_lag, max_lag + 1).astype(jnp.float32).reshape((lag_total,) + (1,) * warped.ndim)
    return lax.optimization_barrier(jnp.sum(lag_values * scores, axis=0)) / lax.optimization_barrier(jnp.sum(scores, axis=0))

def reference(gathers, shift_start):
    smoother = ramp_matrix(gathers.shape[-1])
    warped_first = warp_traces(gathers, shift_start)
    stacked_sum = lax.optimization_barrier(jnp.sum(warped_first, axis=0)) / gathers.shape[0]
    pilot_trace = lateral_blur(stacked_sum, 0, 1).astype(jnp.bfloat16)
    pilot_square = jnp.square(pilot_trace.astype(jnp.float32)).astype(jnp.bfloat16)
    pilot_energy = wide_rows(pilot_square.reshape(-1, pilot_square.shape[-1]), smoother).reshape(pilot_square.shape)
    warped = warped_first.astype(jnp.bfloat16)
    shifts = shift_start
    for iteration in range(ITERS):
        update_field = lax.map(lambda traces: shift_update(traces, pilot_trace, pilot_energy, smoother, wide_rows), warped)
        shifts = shift_limit * jnp.tanh((shifts + lateral_blur(update_field, 1, 2)) / shift_limit)
        if iteration + 1 < ITERS:
            warped = warp_traces(gathers, shifts).astype(jnp.bfloat16)
    return shifts
```

```python
import functools

import jax
import jax.numpy as jnp
from jax import lax
from jax.experimental import pallas as pl
from jax.experimental.pallas import tpu as pltpu
from jax.sharding import PartitionSpec as P

ITERS = 3
NT = 256
HALF = NT // 2
TAPS = 5
LAGS = 4
NLAG = 2 * LAGS + 1
REACH = 2
RAMP = 40.0
GAIN = 4.0
LIMIT = 2.0
EPS = 1e-05
SIDE = REACH * ITERS
BINOMIAL = (0.0625, 0.25, 0.375, 0.25, 0.0625)

F_POLY = (9.99999968e-01 / 28800, -1.81322370e-01 / 28800, 1.54516284e-02 / 28800,
          -8.25726533e-04 / 28800, 3.04896991e-05 / 28800, -6.88441806e-07 / 28800)
C_POLY = (1.0, -1.37077839e-01, 3.13172223e-03, -2.86192176e-05, 1.40062638e-07, -4.16282303e-10)
S_POLY = (5.23598776e-01, -2.39245957e-02, 3.27952196e-04, -2.14001963e-06, 7.95044038e-09)
COS1 = 0.8660254037844386


def horner(coefs, x):
    total = coefs[-1]
    for c in coefs[-2::-1]:
        total = total * x + c
    return total


def lane_index(rows):
    return lax.broadcasted_iota(jnp.int32, (rows, HALF), 1)


def shifted(a, b, k, lane):
    if k == 0:
        return a, b
    zero = jnp.zeros_like(a)
    if k > 0:
        ra = pltpu.roll(a, HALF - k, 1)
        rb = pltpu.roll(b, HALF - k, 1)
        keep = lane < HALF - k
        return jnp.where(keep, ra, rb), jnp.where(keep, rb, zero)
    ra = pltpu.roll(a, -k, 1)
    rb = pltpu.roll(b, -k, 1)
    keep = lane >= -k
    return jnp.where(keep, ra, zero), jnp.where(keep, rb, ra)


def tap_weights(s):
    x = s * s
    f = horner(F_POLY, x)
    c = horner(C_POLY, x)
    q = horner(S_POLY, x)
    sn = s * q
    ss = x * q
    sc = s * c
    n1, n4, n9, n16, n25 = 1.0 - x, 4.0 - x, 9.0 - x, 16.0 - x, 25.0 - x
    h = s * f
    d = n1 * n4
    e = n9 * n16
    k2 = n25 * h
    k3 = e * k2
    k4 = d * k2
    facs = (n4 * k3, -(n1 * k3), n16 * k4, -(n9 * k4), (d * e) * h)
    w0 = ((d * e) * (n25 * f)) * (1.0 + c)
    u1, v1, v2 = COS1 * c, 0.5 * ss, COS1 * ss
    y1, y2, z1, z2 = COS1 * sc, 0.5 * sc, 0.5 * sn, COS1 * sn
    firsts = (1.0 + u1 + v1, 2.0 + c + v2, 3.0 + ss, 4.0 - 2.0 * c + v2, 5.0 - 5.0 * u1 + v1)
    seconds = (s + y1 + z1, s + y2 + 2.0 * z2, s + 3.0 * sn, s - y2 + 4.0 * z2, s - y1 + 5.0 * z1)
    return w0, facs, firsts, seconds


def warp_block(ga, gb, sa, sb, lane):
    outs = []
    pairs = [(shifted(ga, gb, j, lane), shifted(ga, gb, -j, lane)) for j in range(1, TAPS + 1)]
    for half, (g, s) in enumerate(((ga, sa), (gb, sb))):
        w0, facs, firsts, seconds = tap_weights(s)
        total = w0 * g
        for j in range(1, TAPS + 1):
            plus = pairs[j - 1][0][half]
            minus = pairs[j - 1][1][half]
            if j == TAPS:
                plus = jnp.where(s > -1.0, plus, 0.0)
                minus = jnp.where(s < 1.0, minus, 0.0)
            f, t = firsts[j - 1], seconds[j - 1]
            total = total + facs[j - 1] * (f * (plus - minus) + t * (plus + minus))
        outs.append(total)
    return outs


def round_bf16(v):
    return v.astype(jnp.bfloat16).astype(jnp.float32)


def halves(ref, rows):
    return ref[rows, 0:HALF], ref[rows, HALF:NT]


def first_kernel(g_ref, s_ref, gs_ref, left_ref, right_ref, w_ref, part_ref, wide_ga, wide_gb, wide_sa, wide_sb):
    noff, nrow, ncol = 4, 8, 16

    def widen(i, _):
        r = pl.ds(pl.multiple_of(i * 32, 32), 32)
        g = g_ref[r, :].astype(jnp.float32)
        wide_ga[r, :] = g[:, 0:HALF]
        wide_gb[r, :] = g[:, HALF:NT]
        wide_sa[r, :] = s_ref[r, 0:HALF]
        wide_sb[r, :] = s_ref[r, HALF:NT]
        return 0

    lax.fori_loop(0, noff * nrow * ncol // 32, widen, 0)
    lane = lane_index(16)

    def body(cp, _):
        acc = [jnp.zeros((16, HALF), jnp.float32)] * 2
        for o in range(noff):
            parts = []
            for src in (wide_ga, wide_gb, wide_sa, wide_sb):
                tiles = [src[pl.ds(o * nrow * ncol + 2 * cp + k, nrow, stride=ncol), :] for k in range(2)]
                parts.append(jnp.concatenate(tiles, axis=0))
            ga, gb, sa, sb = parts
            row = pl.ds(pl.multiple_of(o * 128 + cp * 16, 16), 16)
            gs_ref[0, row, 0:HALF] = ga
            gs_ref[0, row, HALF:NT] = gb
            gs_ref[1, row, 0:HALF] = sa
            gs_ref[1, row, HALF:NT] = sb
            wa, wb = warp_block(ga, gb, sa, sb, lane)
            w_ref[row, 0:HALF] = wa.astype(jnp.bfloat16)
            w_ref[row, HALF:NT] = wb.astype(jnp.bfloat16)
            acc = [acc[0] + wa, acc[1] + wb]
        row = pl.ds(pl.multiple_of(cp * 16, 16), 16)
        part_ref[row, 0:HALF] = acc[0]
        part_ref[row, HALF:NT] = acc[1]
        return 0

    lax.fori_loop(0, ncol // 2, body, 0)
    n = SIDE * 8
    for k in range(2):
        for o in range(noff):
            left_ref[k, o * n:(o + 1) * n, :] = gs_ref[k, o * 128:o * 128 + n, :]
            right_ref[k, o * n:(o + 1) * n, :] = gs_ref[k, o * 128 + 128 - n:o * 128 + 128, :]


def pack_edges(src, ngroup, odd, send_a, send_b, narrow):
    sub = lax.broadcasted_iota(jnp.int32, (8, NT), 0) // 2

    def tiles(base):
        top = bottom = None
        for k in range(4):
            t = src[pl.ds(pl.multiple_of(base + 8 * k, 8), 8), :]
            u = t if k == 0 else pltpu.roll(t, 2 * k, 0)
            d = t if k == 3 else pltpu.roll(t, 2 * k + 2, 0)
            top = u if k == 0 else jnp.where(sub == k, u, top)
            bottom = d if k == 0 else jnp.where(sub == k, d, bottom)
        flag = odd != 0
        return jnp.where(flag, bottom, top), jnp.where(flag, top, bottom)

    if narrow:
        def body(i, _):
            a0, b0 = tiles(i * 64)
            a1, b1 = tiles(i * 64 + 32)
            r = pl.ds(pl.multiple_of(i * 16, 16), 16)
            send_a[r, :] = jnp.concatenate([a0, a1], axis=0).astype(jnp.bfloat16)
            send_b[r, :] = jnp.concatenate([b0, b1], axis=0).astype(jnp.bfloat16)
            return 0
        lax.fori_loop(0, ngroup // 2, body, 0)
    else:
        def body(i, _):
            a, b = tiles(i * 32)
            r = pl.ds(pl.multiple_of(i * 8, 8), 8)
            send_a[r, :] = a
            send_b[r, :] = b
            return 0
        lax.fori_loop(0, ngroup, body, 0)


def blur_rows(src, ngroup, odd, recv_a, recv_b, dst, narrow):
    sub = lax.broadcasted_iota(jnp.int32, (8, NT), 0)
    flag = odd != 0

    def tile4(base, ra, rb):
        below = jnp.where(flag, ra, rb)
        above = jnp.where(flag, rb, ra)
        for k in range(4):
            r = pl.ds(pl.multiple_of(base + 8 * k, 8), 8)
            cur = src[r, :]
            dn = below if k == 0 else pltpu.roll(below, 8 - 2 * k, 0)
            up = above if k == 3 else pltpu.roll(above, 6 - 2 * k, 0)
            h = jnp.where(sub < 4, dn, up)
            p1 = pltpu.roll(jnp.where(sub >= 1, cur, h), 7, 0)
            p2 = pltpu.roll(jnp.where(sub >= 2, cur, h), 6, 0)
            m1 = pltpu.roll(jnp.where(sub <= 6, cur, h), 1, 0)
            m2 = pltpu.roll(jnp.where(sub <= 5, cur, h), 2, 0)
            dst[r, :] = BINOMIAL[2] * cur + BINOMIAL[1] * (p1 + m1) + BINOMIAL[0] * (p2 + m2)

    if narrow:
        def body(i, _):
            r = pl.ds(pl.multiple_of(i * 16, 16), 16)
            ra = recv_a[r, :].astype(jnp.float32)
            rb = recv_b[r, :].astype(jnp.float32)
            tile4(i * 64, ra[0:8], rb[0:8])
            tile4(i * 64 + 32, ra[8:16], rb[8:16])
            return 0
        lax.fori_loop(0, ngroup // 2, body, 0)
    else:
        def body(i, _):
            r = pl.ds(pl.multiple_of(i * 8, 8), 8)
            tile4(i * 32, recv_a[r, :], recv_b[r, :])
            return 0
        lax.fori_loop(0, ngroup, body, 0)


def blur_cols(src, start, rows):
    total = None
    for k, w in enumerate(BINOMIAL):
        v = src[pl.ds(pl.multiple_of(start + 8 * k, 8), rows), :]
        total = w * v if total is None else total + w * v
    return total


def stack_kernel(odd_ref, mine_ref, other_ref, stack_ref, a_ref, b_ref, *, scale):
    stack_ref[...] = (mine_ref[...] + other_ref[...]) * scale
    pack_edges(stack_ref, 4, odd_ref[0], a_ref, b_ref, False)


def stack_blur_kernel(odd_ref, stack_ref, a_ref, b_ref, out_ref):
    blur_rows(stack_ref, 4, odd_ref[0], a_ref, b_ref, out_ref, False)


def store_products(wa, wb, pa, pb, rows, prod, ener, lane):
    ener[rows, 0:HALF] = (wa * wa).astype(jnp.bfloat16)
    ener[rows, HALF:NT] = (wb * wb).astype(jnp.bfloat16)
    for l in range(NLAG):
        va, vb = shifted(wa, wb, l - LAGS, lane)
        prod[l, rows, 0:HALF] = (pa * va).astype(jnp.bfloat16)
        prod[l, rows, HALF:NT] = (pb * vb).astype(jnp.bfloat16)


def correlate(ncol, prod, ener, smooth_ref, lagged_ref, corr, lage, pe_ref, pe_skip, u_ref):
    total = 4 * ncol * 8

    def dots(l, _):
        corr[l, 0:total, :] = jnp.dot(prod[l, 0:total, :], smooth_ref[...], preferred_element_type=jnp.float32)
        lage[l, 0:total, :] = jnp.dot(ener[0:total, :], lagged_ref[l], preferred_element_type=jnp.float32)
        return 0

    lax.fori_loop(0, NLAG, dots, 0)

    def offset(o, _):
        def body(cp, _):
            r = pl.ds(pl.multiple_of(o * ncol * 8 + cp * 16, 16), 16)
            pr = pl.ds(pl.multiple_of(pe_skip * 8 + cp * 16, 8), 16)
            for lo in (0, HALF):
                t = pl.ds(lo, HALF)
                pe = pe_ref[pr, t]
                den = num = None
                for l in range(NLAG):
                    coh = corr[l, r, t] * lax.rsqrt(pe * lage[l, r, t] + EPS)
                    score = jnp.exp(GAIN * coh)
                    den = score if den is None else den + score
                    if l != LAGS:
                        term = float(l - LAGS) * score
                        num = term if num is None else num + term
                u_ref[r, t] = num / den
            return 0

        lax.fori_loop(0, ncol // 2, body, 0)
        return 0

    lax.fori_loop(0, 4, offset, 0)


def pilot_kernel(odd_ref, v_ref, vl_ref, vr_ref, gs_ref, w_ref, hl_ref, hr_ref, smooth_ref, lagged_ref,
                 g_out, s_out, pilot_ref, pe_ref, u_ref, a_ref, b_ref, vext, prod, ener, corr, lage):
    ncol = 16 + 2 * SIDE
    vext[0:64, :] = vl_ref[...]
    vext[64:192, :] = v_ref[...]
    vext[192:256, :] = vr_ref[...]

    def make_pilot(i, _):
        r = pl.ds(pl.multiple_of(i * 16, 16), 16)
        pilot_ref[r, :] = round_bf16(blur_cols(vext, i * 16, 16))
        return 0

    lax.fori_loop(0, ncol // 2, make_pilot, 0)
    sq = jnp.square(pilot_ref[...]).astype(jnp.bfloat16)
    pe_ref[...] = jnp.dot(sq, smooth_ref[...], preferred_element_type=jnp.float32)

    lane = lane_index(16)
    side = SIDE * 8

    def offset(o, _):
        def halo(hp, _):
            for ref, first in ((hl_ref, 0), (hr_ref, ncol - SIDE)):
                src = pl.ds(pl.multiple_of(o * side + hp * 16, 16), 16)
                dst = pl.ds(pl.multiple_of(o * ncol * 8 + first * 8 + hp * 16, 16), 16)
                pr = pl.ds(pl.multiple_of(first * 8 + hp * 16, 16), 16)
                ga, gb = ref[0, src, 0:HALF], ref[0, src, HALF:NT]
                sa, sb = ref[1, src, 0:HALF], ref[1, src, HALF:NT]
                g_out[dst, 0:HALF] = ga
                g_out[dst, HALF:NT] = gb
                s_out[dst, 0:HALF] = sa
                s_out[dst, HALF:NT] = sb
                wa, wb = warp_block(ga, gb, sa, sb, lane)
                pa, pb = halves(pilot_ref, pr)
                store_products(round_bf16(wa), round_bf16(wb), pa, pb, dst, prod, ener, lane)
            return 0

        lax.fori_loop(0, SIDE // 2, halo, 0)

        def own(cp, _):
            src = pl.ds(pl.multiple_of(o * 128 + cp * 16, 16), 16)
            dst = pl.ds(pl.multiple_of(o * ncol * 8 + side + cp * 16, 16), 16)
            pr = pl.ds(pl.multiple_of(side + cp * 16, 16), 16)
            g_out[dst, :] = gs_ref[0, src, :]
            s_out[dst, :] = gs_ref[1, src, :]
            wa = w_ref[src, 0:HALF].astype(jnp.float32)
            wb = w_ref[src, HALF:NT].astype(jnp.float32)
            pa, pb = halves(pilot_ref, pr)
            store_products(wa, wb, pa, pb, dst, prod, ener, lane)
            return 0

        lax.fori_loop(0, 8, own, 0)
        return 0

    lax.fori_loop(0, 4, offset, 0)
    correlate(ncol, prod, ener, smooth_ref, lagged_ref, corr, lage, pe_ref, 0, u_ref)
    pack_edges(u_ref, ncol, odd_ref[0], a_ref, b_ref, True)


def step_kernel(odd_ref, u_old, ra_ref, rb_ref, s_old, g_ref, pilot_ref, pe_ref, smooth_ref, lagged_ref,
                s_out, u_ref, a_ref, b_ref, vbuf, prod, ener, corr, lage, *, ncol):
    wide = ncol + 4
    skip = (16 + 2 * SIDE - ncol) // 2
    blur_rows(u_old, wide, odd_ref[0], ra_ref, rb_ref, vbuf, True)
    lane = lane_index(16)

    def offset(o, _):
        def body(cp, _):
            src = pl.multiple_of((o * wide) * 8 + cp * 16, 16)
            dst = pl.ds(pl.multiple_of(o * ncol * 8 + cp * 16, 16), 16)
            sr = pl.ds(pl.multiple_of(o * wide * 8 + 16 + cp * 16, 16), 16)
            gr = pl.ds(pl.multiple_of(o * (16 + 2 * SIDE) * 8 + skip * 8 + cp * 16, 16), 16)
            pr = pl.ds(pl.multiple_of(skip * 8 + cp * 16, 16), 16)
            s = LIMIT * jnp.tanh((s_old[sr, :] + blur_cols(vbuf, src, 16)) / LIMIT)
            s_out[dst, :] = s
            ga, gb = halves(g_ref, gr)
            wa, wb = warp_block(ga, gb, s[:, 0:HALF], s[:, HALF:NT], lane)
            pa, pb = halves(pilot_ref, pr)
            store_products(round_bf16(wa), round_bf16(wb), pa, pb, dst, prod, ener, lane)
            return 0

        lax.fori_loop(0, ncol // 2, body, 0)
        return 0

    lax.fori_loop(0, 4, offset, 0)
    correlate(ncol, prod, ener, smooth_ref, lagged_ref, corr, lage, pe_ref, skip, u_ref)
    pack_edges(u_ref, ncol, odd_ref[0], a_ref, b_ref, True)


def last_kernel(odd_ref, u_old, ra_ref, rb_ref, s_old, out_ref, vbuf, out_a, out_b):
    wide = 16 + 4
    blur_rows(u_old, wide, odd_ref[0], ra_ref, rb_ref, vbuf, True)

    def body(i, _):
        o = i // 8
        cp = lax.rem(i, 8)
        src = pl.multiple_of(o * wide * 8 + cp * 16, 16)
        sr = pl.ds(pl.multiple_of(o * wide * 8 + 16 + cp * 16, 16), 16)
        s = LIMIT * jnp.tanh((s_old[sr, :] + blur_cols(vbuf, src, 16)) / LIMIT)
        for k in range(2):
            r = pl.ds(o * 128 + 2 * cp + k, 8, stride=16)
            out_a[r, :] = s[8 * k:8 * k + 8, 0:HALF]
            out_b[r, :] = s[8 * k:8 * k + 8, HALF:NT]
        return 0

    lax.fori_loop(0, 32, body, 0)
    out_ref[:, 0:HALF] = out_a[...]
    out_ref[:, HALF:NT] = out_b[...]


VMEM = pl.BlockSpec(memory_space=pltpu.VMEM)
SMEM = pl.BlockSpec(memory_space=pltpu.SMEM)
F32 = jnp.float32
BF16 = jnp.bfloat16


def call(kernel, args, outs, scratch=(), scalar=True, flops=10**8, name=None):
    shapes = [jax.ShapeDtypeStruct(s, d) for s, d in outs]
    specs = [VMEM] * len(args)
    if scalar:
        specs[0] = SMEM
    return pl.pallas_call(
        kernel,
        out_shape=shapes,
        in_specs=specs,
        out_specs=[VMEM] * len(outs),
        scratch_shapes=[pltpu.VMEM(s, d) for s, d in scratch],
        compiler_params=pltpu.CompilerParams(vmem_limit_bytes=50 * 2**20),
        cost_estimate=pl.CostEstimate(flops=flops, bytes_accessed=2 * 10**6, transcendentals=0),
        name=name,
    )(*args)


def swap(cells, axis, first):
    count = lax.axis_size(axis)
    pairs = []
    for i in range(first, count - 1, 2):
        pairs += [(i, i + 1), (i + 1, i)]
    return lax.ppermute(cells, axis, pairs)


def ship(cells, axis, step):
    count = lax.axis_size(axis)
    return lax.ppermute(cells, axis, [(i, i + step) for i in range(count) if 0 <= i + step < count])


def smoothers():
    w = jnp.arange(NT)[:, None]
    t = jnp.arange(NT)[None, :]

    def ramp(d):
        return jnp.maximum(RAMP - jnp.abs(d).astype(F32), 0.0) / RAMP

    mats = []
    for l in range(-LAGS, LAGS + 1):
        u = w - l
        mats.append(jnp.where((u >= 0) & (u < NT), ramp(u - t), 0.0).astype(BF16))
    return ramp(w - t).astype(BF16), jnp.stack(mats)


def shards(gathers, shift_start):
    odd = lax.rem(lax.axis_index("inl"), 2).astype(jnp.int32).reshape(1)
    smooth, lagged = smoothers()
    rows = 4 * 8 * 16
    side = 4 * SIDE * 8
    gs, to_left, to_right, w_own, part = call(
        first_kernel,
        [gathers.reshape(rows, NT), shift_start.reshape(rows, NT)],
        [((2, rows, NT), F32), ((2, side, NT), F32), ((2, side, NT), F32), ((rows, NT), BF16), ((128, NT), F32)],
        [((rows, HALF), F32)] * 4, scalar=False, name="first",
    )
    part = part + lax.ppermute(part, "off", [(i, i ^ 1) for i in range(8)])
    part = part + lax.ppermute(part, "off", [(i, i ^ 2) for i in range(8)])
    other = lax.ppermute(part, "off", [(i, 2 * (3 - i // 2) + i % 2) for i in range(8)])
    halo_left = ship(to_right, "xl", 1)
    halo_right = ship(to_left, "xl", -1)
    total = 4 * lax.axis_size("off")
    stack, a, b = call(
        functools.partial(stack_kernel, scale=1.0 / total), [odd, part, other],
        [((128, NT), F32), ((32, NT), F32), ((32, NT), F32)], name="stack",
    )
    ra, rb = swap(a, "inl", 1), swap(b, "inl", 0)
    (v,) = call(stack_blur_kernel, [odd, stack, ra, rb], [((128, NT), F32)], name="stackblur")
    vl = ship(v[64:], "xl", 1)
    vr = ship(v[:64], "xl", -1)

    ncol = 16 + 2 * SIDE
    n = 4 * ncol * 8
    work = [((NLAG, n, NT), BF16), ((n, NT), BF16), ((NLAG, n, NT), F32), ((NLAG, n, NT), F32)]
    g_ext, s_ext, pilot, pe, u, a, b = call(
        pilot_kernel, [odd, v, vl, vr, gs, w_own, halo_left, halo_right, smooth, lagged],
        [((n, NT), F32), ((n, NT), F32), ((ncol * 8, NT), F32), ((ncol * 8, NT), F32), ((n, NT), F32),
         ((n // 4, NT), BF16), ((n // 4, NT), BF16)],
        [((256, NT), F32)] + work, name="pilot",
    )
    for _ in range(ITERS - 1):
        ra, rb = swap(a, "inl", 1), swap(b, "inl", 0)
        ncol -= 4
        n = 4 * ncol * 8
        work = [((NLAG, n, NT), BF16), ((n, NT), BF16), ((NLAG, n, NT), F32), ((NLAG, n, NT), F32)]
        s_ext, u, a, b = call(
            functools.partial(step_kernel, ncol=ncol),
            [odd, u, ra, rb, s_ext, g_ext, pilot, pe, smooth, lagged],
            [((n, NT), F32), ((n, NT), F32), ((n // 4, NT), BF16), ((n // 4, NT), BF16)],
            [((4 * (ncol + 4) * 8, NT), F32)] + work, name="step%d" % ncol,
        )
    ra, rb = swap(a, "inl", 1), swap(b, "inl", 0)
    (out,) = call(last_kernel, [odd, u, ra, rb, s_ext], [((rows, NT), F32)],
                  [((n, NT), F32), ((rows, HALF), F32), ((rows, HALF), F32)], name="last")
    return out.reshape(shift_start.shape)


def solution(mesh):
    spec = P("off", "inl", "xl", None)
    return jax.shard_map(shards, mesh=mesh, in_specs=(spec, spec), out_specs=spec, check_vma=False)
```

```python
import functools

import jax
import jax.numpy as jnp
from jax import lax
from jax.experimental import pallas as pl
from jax.experimental.pallas import tpu as pltpu
from jax.sharding import PartitionSpec as P

ITERS = 3
NT = 256
HALF = NT // 2
TAPS = 5
LAGS = 4
NLAG = 2 * LAGS + 1
REACH = 2
RAMP = 40.0
GAIN = 4.0
LIMIT = 2.0
EPS = 1e-05
SIDE = REACH * ITERS
BINOMIAL = (0.0625, 0.25, 0.375, 0.25, 0.0625)

F_POLY = (9.99999968e-01 / 28800, -1.81322370e-01 / 28800, 1.54516284e-02 / 28800,
          -8.25726533e-04 / 28800, 3.04896991e-05 / 28800, -6.88441806e-07 / 28800)
C_POLY = (1.0, -1.37077839e-01, 3.13172223e-03, -2.86192176e-05, 1.40062638e-07, -4.16282303e-10)
S_POLY = (5.23598776e-01, -2.39245957e-02, 3.27952196e-04, -2.14001963e-06, 7.95044038e-09)
COS1 = 0.8660254037844386


def horner(coefs, x):
    total = coefs[-1]
    for c in coefs[-2::-1]:
        total = total * x + c
    return total


def lane_index(rows):
    return lax.broadcasted_iota(jnp.int32, (rows, HALF), 1)


def shifted(a, b, k, lane):
    if k == 0:
        return a, b
    zero = jnp.zeros_like(a)
    if k > 0:
        ra = pltpu.roll(a, HALF - k, 1)
        rb = pltpu.roll(b, HALF - k, 1)
        keep = lane < HALF - k
        return jnp.where(keep, ra, rb), jnp.where(keep, rb, zero)
    ra = pltpu.roll(a, -k, 1)
    rb = pltpu.roll(b, -k, 1)
    keep = lane >= -k
    return jnp.where(keep, ra, zero), jnp.where(keep, rb, ra)


def tap_weights(s):
    x = s * s
    f = horner(F_POLY, x)
    c = horner(C_POLY, x)
    q = horner(S_POLY, x)
    sn = s * q
    ss = x * q
    sc = s * c
    n1, n4, n9, n16, n25 = 1.0 - x, 4.0 - x, 9.0 - x, 16.0 - x, 25.0 - x
    h = s * f
    d = n1 * n4
    e = n9 * n16
    k2 = n25 * h
    k3 = e * k2
    k4 = d * k2
    facs = (n4 * k3, -(n1 * k3), n16 * k4, -(n9 * k4), (d * e) * h)
    w0 = ((d * e) * (n25 * f)) * (1.0 + c)
    u1, v1, v2 = COS1 * c, 0.5 * ss, COS1 * ss
    y1, y2, z1, z2 = COS1 * sc, 0.5 * sc, 0.5 * sn, COS1 * sn
    firsts = (1.0 + u1 + v1, 2.0 + c + v2, 3.0 + ss, 4.0 - 2.0 * c + v2, 5.0 - 5.0 * u1 + v1)
    seconds = (s + y1 + z1, s + y2 + 2.0 * z2, s + 3.0 * sn, s - y2 + 4.0 * z2, s - y1 + 5.0 * z1)
    return w0, facs, firsts, seconds


def warp_block(ga, gb, sa, sb, lane):
    outs = []
    pairs = [(shifted(ga, gb, j, lane), shifted(ga, gb, -j, lane)) for j in range(1, TAPS + 1)]
    for half, (g, s) in enumerate(((ga, sa), (gb, sb))):
        w0, facs, firsts, seconds = tap_weights(s)
        total = w0 * g
        for j in range(1, TAPS + 1):
            plus = pairs[j - 1][0][half]
            minus = pairs[j - 1][1][half]
            if j == TAPS:
                plus = jnp.where(s > -1.0, plus, 0.0)
                minus = jnp.where(s < 1.0, minus, 0.0)
            f, t = firsts[j - 1], seconds[j - 1]
            total = total + facs[j - 1] * (f * (plus - minus) + t * (plus + minus))
        outs.append(total)
    return outs


def halves(ref, rows):
    return ref[rows, 0:HALF], ref[rows, HALF:NT]


def first_kernel(g_hbm, s_hbm, gs_ref, left_ref, right_ref, w_ref, part_ref,
                 g_in, s_in, wide_ga, wide_gb, wide_sa, wide_sb, g_sem, s_sem):
    noff, nrow, ncol = 4, 8, 16
    n = nrow * ncol

    def copies(o):
        return (pltpu.make_async_copy(g_hbm.at[o], g_in.at[o], g_sem.at[o]),
                pltpu.make_async_copy(s_hbm.at[o], s_in.at[o], s_sem.at[o]))

    for o in range(noff):
        for c in copies(o):
            c.start()
    lane = lane_index(16)
    side = SIDE * 8

    for o in range(noff):
        for c in copies(o):
            c.wait()
        g = g_in[o].astype(jnp.float32)
        wide_ga[...] = g[:, 0:HALF]
        wide_gb[...] = g[:, HALF:NT]
        wide_sa[...] = s_in[o, :, 0:HALF]
        wide_sb[...] = s_in[o, :, HALF:NT]

        def body(i, _):
            for q in range(2):
                cp = 2 * i + q
                parts = []
                for src in (wide_ga, wide_gb, wide_sa, wide_sb):
                    tiles = [src[pl.ds(2 * cp + k, nrow, stride=ncol), :] for k in range(2)]
                    parts.append(jnp.concatenate(tiles, axis=0))
                ga, gb, sa, sb = parts
                row = pl.ds(pl.multiple_of(o * n + cp * 16, 16), 16)
                gs_ref[0, row, 0:HALF] = ga
                gs_ref[0, row, HALF:NT] = gb
                gs_ref[1, row, 0:HALF] = sa
                gs_ref[1, row, HALF:NT] = sb
                wa, wb = warp_block(ga, gb, sa, sb, lane)
                w_ref[row, 0:HALF] = wa.astype(jnp.bfloat16)
                w_ref[row, HALF:NT] = wb.astype(jnp.bfloat16)
                prow = pl.ds(pl.multiple_of(cp * 16, 16), 16)
                if o == 0:
                    part_ref[prow, 0:HALF] = wa
                    part_ref[prow, HALF:NT] = wb
                else:
                    part_ref[prow, 0:HALF] += wa
                    part_ref[prow, HALF:NT] += wb
            return 0

        lax.fori_loop(0, ncol // 4, body, 0)
        for k in range(2):
            left_ref[k, o * side:(o + 1) * side, :] = gs_ref[k, o * n:o * n + side, :]
            right_ref[k, o * side:(o + 1) * side, :] = gs_ref[k, o * n + n - side:o * n + n, :]


def pack_edges(src, ngroup, odd, send_a, send_b, narrow):
    sub = lax.broadcasted_iota(jnp.int32, (8, NT), 0) // 2

    def tiles(base):
        top = bottom = None
        for k in range(4):
            t = src[pl.ds(pl.multiple_of(base + 8 * k, 8), 8), :]
            u = t if k == 0 else pltpu.roll(t, 2 * k, 0)
            d = t if k == 3 else pltpu.roll(t, 2 * k + 2, 0)
            top = u if k == 0 else jnp.where(sub == k, u, top)
            bottom = d if k == 0 else jnp.where(sub == k, d, bottom)
        flag = odd != 0
        return jnp.where(flag, bottom, top), jnp.where(flag, top, bottom)

    if narrow:
        def body(i, _):
            a0, b0 = tiles(i * 64)
            a1, b1 = tiles(i * 64 + 32)
            r = pl.ds(pl.multiple_of(i * 16, 16), 16)
            send_a[r, :] = jnp.concatenate([a0, a1], axis=0).astype(jnp.bfloat16)
            send_b[r, :] = jnp.concatenate([b0, b1], axis=0).astype(jnp.bfloat16)
            return 0
        lax.fori_loop(0, ngroup // 2, body, 0)
    else:
        def body(i, _):
            a, b = tiles(i * 32)
            r = pl.ds(pl.multiple_of(i * 8, 8), 8)
            send_a[r, :] = a
            send_b[r, :] = b
            return 0
        lax.fori_loop(0, ngroup, body, 0)


def blur_rows(src, ngroup, odd, recv_a, recv_b, dst, narrow):
    sub = lax.broadcasted_iota(jnp.int32, (8, NT), 0)
    flag = odd != 0

    def tile4(base, ra, rb):
        below = jnp.where(flag, ra, rb)
        above = jnp.where(flag, rb, ra)
        for k in range(4):
            r = pl.ds(pl.multiple_of(base + 8 * k, 8), 8)
            cur = src[r, :]
            dn = below if k == 0 else pltpu.roll(below, 8 - 2 * k, 0)
            up = above if k == 3 else pltpu.roll(above, 6 - 2 * k, 0)
            h = jnp.where(sub < 4, dn, up)
            p1 = pltpu.roll(jnp.where(sub >= 1, cur, h), 7, 0)
            p2 = pltpu.roll(jnp.where(sub >= 2, cur, h), 6, 0)
            m1 = pltpu.roll(jnp.where(sub <= 6, cur, h), 1, 0)
            m2 = pltpu.roll(jnp.where(sub <= 5, cur, h), 2, 0)
            dst[r, :] = BINOMIAL[2] * cur + BINOMIAL[1] * (p1 + m1) + BINOMIAL[0] * (p2 + m2)

    if narrow:
        def body(i, _):
            r = pl.ds(pl.multiple_of(i * 16, 16), 16)
            ra = recv_a[r, :].astype(jnp.float32)
            rb = recv_b[r, :].astype(jnp.float32)
            tile4(i * 64, ra[0:8], rb[0:8])
            tile4(i * 64 + 32, ra[8:16], rb[8:16])
            return 0
        lax.fori_loop(0, ngroup // 2, body, 0)
    else:
        def body(i, _):
            r = pl.ds(pl.multiple_of(i * 8, 8), 8)
            tile4(i * 32, recv_a[r, :], recv_b[r, :])
            return 0
        lax.fori_loop(0, ngroup, body, 0)


def blur_cols(src, start, rows):
    total = None
    for k, w in enumerate(BINOMIAL):
        v = src[pl.ds(pl.multiple_of(start + 8 * k, 8), rows), :]
        total = w * v if total is None else total + w * v
    return total


def stack_kernel(odd_ref, mine_ref, other_ref, stack_ref, a_ref, b_ref, *, scale):
    stack_ref[...] = (mine_ref[...] + other_ref[...].astype(jnp.float32)) * scale
    pack_edges(stack_ref, 4, odd_ref[0], a_ref, b_ref, False)


def stack_blur_kernel(odd_ref, stack_ref, a_ref, b_ref, out_ref):
    blur_rows(stack_ref, 4, odd_ref[0], a_ref, b_ref, out_ref, False)


SCALE = GAIN * 1.4426950408889634
BLOCK = 32


def store_products(wa, wb, pa, pb, first, buf, lane):
    ea, eb = wa * wa, wb * wb
    for l in range(NLAG):
        va, vb = shifted(wa, wb, l - LAGS, lane)
        r = l * BLOCK + first
        buf[r:r + 16, 0:HALF] = pa * va
        buf[r:r + 16, HALF:NT] = pb * vb
        va, vb = shifted(ea, eb, l - LAGS, lane)
        r += NLAG * BLOCK
        buf[r:r + 16, 0:HALF] = va
        buf[r:r + 16, HALF:NT] = vb


def finish_update(buf, smooth_ref, pe_ref, pe_row, u_ref, u_row):
    sums = jnp.dot(buf[...], smooth_ref[...], preferred_element_type=jnp.float32)
    for first in range(0, BLOCK, 16):
        for lo in (0, HALF):
            pe = pe_ref[pl.ds(pl.multiple_of(pe_row + first, 16), 16), lo:lo + HALF]
            scores = []
            for l in range(NLAG):
                r = l * BLOCK + first
                co = sums[r:r + 16, lo:lo + HALF]
                r += NLAG * BLOCK
                le = sums[r:r + 16, lo:lo + HALF]
                scores.append(jnp.exp2(co * lax.rsqrt(pe * le + EPS / SCALE**2)))
            den = scores[LAGS]
            run = num = None
            for k in range(LAGS, 0, -1):
                up, down = scores[LAGS + k], scores[LAGS - k]
                den = den + (up + down)
                run = up - down if run is None else run + (up - down)
                num = run if num is None else num + run
            u_ref[pl.ds(pl.multiple_of(u_row + first, 16), 16), lo:lo + HALF] = num / den


def pipeline(ncol, prepare, finish):
    per = ncol // 4
    prepare(0, 0)

    def body(i, _):
        j = i - 1
        finish(j, lax.rem(j, per))
        prepare(i // per, lax.rem(i, per))
        return 0

    lax.fori_loop(1, 4 * per, body, 0)
    finish(4 * per - 1, per - 1)


def halo_kernel(gs_ref, w_ref, hl_ref, hr_ref, g_out, s_out, w_out):
    ncol = 16 + 2 * SIDE
    lane = lane_index(16)
    side = SIDE * 8
    for o in range(4):
        n = o * ncol * 8
        m = o * 128
        g_out[n + side:n + side + 128, :] = gs_ref[0, m:m + 128, :]
        s_out[n + side:n + side + 128, :] = gs_ref[1, m:m + 128, :]
        w_out[n + side:n + side + 128, :] = w_ref[m:m + 128, :]

    def body(i, _):
        o = i // (SIDE // 2)
        hp = lax.rem(i, SIDE // 2)
        src = pl.ds(pl.multiple_of(i * 16, 16), 16)
        for ref, first in ((hl_ref, 0), (hr_ref, ncol - SIDE)):
            dst = pl.ds(pl.multiple_of(o * ncol * 8 + first * 8 + hp * 16, 16), 16)
            ga, gb = ref[0, src, 0:HALF], ref[0, src, HALF:NT]
            sa, sb = ref[1, src, 0:HALF], ref[1, src, HALF:NT]
            g_out[dst, 0:HALF] = ga
            g_out[dst, HALF:NT] = gb
            s_out[dst, 0:HALF] = sa
            s_out[dst, HALF:NT] = sb
            wa, wb = warp_block(ga, gb, sa, sb, lane)
            w_out[dst, 0:HALF] = wa.astype(jnp.bfloat16)
            w_out[dst, HALF:NT] = wb.astype(jnp.bfloat16)
        return 0

    lax.fori_loop(0, 4 * SIDE // 2, body, 0)


def pilot_kernel(odd_ref, v_ref, vl_ref, vr_ref, w_ref, smooth_ref,
                 pilot_ref, pe_ref, u_ref, a_ref, b_ref, vext, buf):
    ncol = 16 + 2 * SIDE
    vext[0:64, :] = vl_ref[...]
    vext[64:192, :] = v_ref[...]
    vext[192:256, :] = vr_ref[...]

    def make_pilot(i, _):
        r = pl.ds(pl.multiple_of(i * 16, 16), 16)
        pilot_ref[r, :] = blur_cols(vext, i * 16, 16).astype(jnp.bfloat16)
        return 0

    lax.fori_loop(0, ncol // 2, make_pilot, 0)
    sq = jnp.square(pilot_ref[...].astype(jnp.float32)).astype(jnp.bfloat16)
    pe_ref[...] = jnp.dot(sq, smooth_ref[...], preferred_element_type=jnp.float32) * (1.0 / SCALE**2)

    lane = lane_index(16)

    def prepare(o, q):
        for first in range(0, BLOCK, 16):
            wr = pl.ds(pl.multiple_of(o * ncol * 8 + q * BLOCK + first, 16), 16)
            pr = pl.ds(pl.multiple_of(q * BLOCK + first, 16), 16)
            wa, wb = halves(w_ref, wr)
            pa, pb = halves(pilot_ref, pr)
            store_products(wa, wb, pa, pb, first, buf, lane)

    def finish(j, q):
        finish_update(buf, smooth_ref, pe_ref, q * BLOCK, u_ref, j * BLOCK)

    pipeline(ncol, prepare, finish)
    pack_edges(u_ref, ncol, odd_ref[0], a_ref, b_ref, True)


def step_kernel(odd_ref, u_old, ra_ref, rb_ref, s_old, g_ref, pilot_ref, pe_ref, smooth_ref,
                s_out, u_ref, a_ref, b_ref, vbuf, buf, *, ncol):
    wide = ncol + 4
    skip = (16 + 2 * SIDE - ncol) // 2
    blur_rows(u_old, wide, odd_ref[0], ra_ref, rb_ref, vbuf, True)
    lane = lane_index(16)

    def prepare(o, q):
        for first in range(0, BLOCK, 16):
            row = q * BLOCK + first
            src = o * wide * 8 + row
            dst = pl.ds(pl.multiple_of(o * ncol * 8 + row, 16), 16)
            sr = pl.ds(pl.multiple_of(src + 16, 16), 16)
            gr = pl.ds(pl.multiple_of(o * (16 + 2 * SIDE) * 8 + skip * 8 + row, 16), 16)
            pr = pl.ds(pl.multiple_of(skip * 8 + row, 16), 16)
            s = LIMIT * jnp.tanh((s_old[sr, :] + blur_cols(vbuf, src, 16)) / LIMIT)
            s_out[dst, :] = s
            ga, gb = halves(g_ref, gr)
            wa, wb = warp_block(ga, gb, s[:, 0:HALF], s[:, HALF:NT], lane)
            pa, pb = halves(pilot_ref, pr)
            store_products(wa.astype(jnp.bfloat16), wb.astype(jnp.bfloat16), pa, pb, first, buf, lane)

    def finish(j, q):
        finish_update(buf, smooth_ref, pe_ref, skip * 8 + q * BLOCK, u_ref, j * BLOCK)

    pipeline(ncol, prepare, finish)
    pack_edges(u_ref, ncol, odd_ref[0], a_ref, b_ref, True)


def last_kernel(odd_ref, u_old, ra_ref, rb_ref, s_old, out_hbm, vbuf, out_a, out_b, out, sem):
    wide = 16 + 4
    blur_rows(u_old, wide, odd_ref[0], ra_ref, rb_ref, vbuf, True)

    def copy(o):
        return pltpu.make_async_copy(out.at[o], out_hbm.at[o], sem.at[o])

    def body(o, _):
        for cp in range(8):
            src = pl.multiple_of(o * wide * 8 + cp * 16, 16)
            sr = pl.ds(pl.multiple_of(o * wide * 8 + 16 + cp * 16, 16), 16)
            s = LIMIT * jnp.tanh((s_old[sr, :] + blur_cols(vbuf, src, 16)) / LIMIT)
            for k in range(2):
                r = pl.ds(2 * cp + k, 8, stride=16)
                out_a[r, :] = s[8 * k:8 * k + 8, 0:HALF]
                out_b[r, :] = s[8 * k:8 * k + 8, HALF:NT]
        out[o, :, 0:HALF] = out_a[...]
        out[o, :, HALF:NT] = out_b[...]
        copy(o).start()
        return 0

    lax.fori_loop(0, 4, body, 0)
    for o in range(4):
        copy(o).wait()


VMEM = pl.BlockSpec(memory_space=pltpu.VMEM)
SMEM = pl.BlockSpec(memory_space=pltpu.SMEM)
HBM = pl.BlockSpec(memory_space=pltpu.HBM)
DMA = pltpu.SemaphoreType.DMA
F32 = jnp.float32
BF16 = jnp.bfloat16


def call(kernel, args, outs, scratch=(), ins=None, out_specs=None, flops=10**8, name=None):
    return pl.pallas_call(
        kernel,
        out_shape=[jax.ShapeDtypeStruct(s, d) for s, d in outs],
        in_specs=ins or [SMEM] + [VMEM] * (len(args) - 1),
        out_specs=out_specs or [VMEM] * len(outs),
        scratch_shapes=[pltpu.VMEM(*s) if isinstance(s, tuple) else s for s in scratch],
        compiler_params=pltpu.CompilerParams(vmem_limit_bytes=16 * 2**20),
        cost_estimate=pl.CostEstimate(flops=flops, bytes_accessed=2 * 10**6, transcendentals=0),
        name=name,
    )(*args)


def swap(cells, axis, first):
    count = lax.axis_size(axis)
    pairs = []
    for i in range(first, count - 1, 2):
        pairs += [(i, i + 1), (i + 1, i)]
    return lax.ppermute(cells, axis, pairs)


def ship(cells, axis, step):
    count = lax.axis_size(axis)
    return lax.ppermute(cells, axis, [(i, i + step) for i in range(count) if 0 <= i + step < count])


def smoother():
    d = jnp.abs(jnp.arange(NT)[:, None] - jnp.arange(NT)[None, :]).astype(F32)
    return (jnp.maximum(RAMP - d, 0.0) / RAMP).astype(BF16)


def shards(gathers, shift_start):
    odd = lax.rem(lax.axis_index("inl"), 2).astype(jnp.int32).reshape(1)
    smooth = smoother()
    rows = 4 * 8 * 16
    side = 4 * SIDE * 8
    gs, to_left, to_right, w_own, part = call(
        first_kernel,
        [gathers.reshape(4, 128, NT), shift_start.reshape(4, 128, NT)],
        [((2, rows, NT), F32), ((2, side, NT), F32), ((2, side, NT), F32), ((rows, NT), BF16), ((128, NT), F32)],
        [((4, 128, NT), BF16), ((4, 128, NT), F32)] + [((128, HALF), F32)] * 4 + [DMA((4,)), DMA((4,))],
        ins=[HBM, HBM], name="first",
    )
    part = part + lax.ppermute(part, "off", [(i, i ^ 1) for i in range(8)])
    part = part + lax.ppermute(part.astype(BF16), "off", [(i, i ^ 2) for i in range(8)]).astype(F32)
    other = lax.ppermute(part.astype(BF16), "off", [(i, 2 * (3 - i // 2) + i % 2) for i in range(8)])
    halo_left = ship(to_right, "xl", 1)
    halo_right = ship(to_left, "xl", -1)
    total = 4 * lax.axis_size("off")
    stack, a, b = call(
        functools.partial(stack_kernel, scale=1.0 / total), [odd, part, other],
        [((128, NT), F32), ((32, NT), F32), ((32, NT), F32)], name="stack",
    )
    ra, rb = swap(a, "inl", 1), swap(b, "inl", 0)
    (v,) = call(stack_blur_kernel, [odd, stack, ra, rb], [((128, NT), F32)], name="stackblur")
    vl = ship(v[64:], "xl", 1)
    vr = ship(v[:64], "xl", -1)

    ncol = 16 + 2 * SIDE
    n = 4 * ncol * 8
    g_ext, s_ext, w_ext = call(
        halo_kernel, [gs, w_own, halo_left, halo_right],
        [((n, NT), F32), ((n, NT), F32), ((n, NT), BF16)], ins=[VMEM] * 4, name="halo",
    )
    work = ((2 * NLAG * BLOCK, NT), BF16)
    pilot, pe, u, a, b = call(
        pilot_kernel, [odd, v, vl, vr, w_ext, smooth],
        [((ncol * 8, NT), BF16), ((ncol * 8, NT), F32), ((n, NT), F32), ((n // 4, NT), BF16), ((n // 4, NT), BF16)],
        [((256, NT), F32), work], name="pilot",
    )
    for _ in range(ITERS - 1):
        ra, rb = swap(a, "inl", 1), swap(b, "inl", 0)
        ncol -= 4
        n = 4 * ncol * 8
        s_ext, u, a, b = call(
            functools.partial(step_kernel, ncol=ncol),
            [odd, u, ra, rb, s_ext, g_ext, pilot, pe, smooth],
            [((n, NT), F32), ((n, NT), F32), ((n // 4, NT), BF16), ((n // 4, NT), BF16)],
            [((4 * (ncol + 4) * 8, NT), F32), work], name="step%d" % ncol,
        )
    ra, rb = swap(a, "inl", 1), swap(b, "inl", 0)
    (out,) = call(
        last_kernel, [odd, u, ra, rb, s_ext], [((4, 128, NT), F32)],
        [((n, NT), F32), ((128, HALF), F32), ((128, HALF), F32), ((4, 128, NT), F32), DMA((4,))],
        out_specs=[HBM], name="last",
    )
    return out.reshape(shift_start.shape)


def solution(mesh):
    spec = P("off", "inl", "xl", None)
    return jax.shard_map(shards, mesh=mesh, in_specs=(spec, spec), out_specs=spec, check_vma=False)
```

```python
import functools

import jax
import jax.numpy as jnp
from jax import lax
from jax.experimental import pallas as pl
from jax.experimental.pallas import tpu as pltpu
from jax.sharding import PartitionSpec as P

ITERS = 3
NT = 256
HALF = NT // 2
TAPS = 5
LAGS = 4
NLAG = 2 * LAGS + 1
REACH = 2
RAMP = 40.0
GAIN = 4.0
LIMIT = 2.0
EPS = 1e-05
SIDE = REACH * ITERS
BINOMIAL = (0.0625, 0.25, 0.375, 0.25, 0.0625)

F_POLY = (9.99999968e-01 / 28800, -1.81322370e-01 / 28800, 1.54516284e-02 / 28800,
          -8.25726533e-04 / 28800, 3.04896991e-05 / 28800, -6.88441806e-07 / 28800)
C_POLY = (1.0, -1.37077839e-01, 3.13172223e-03, -2.86192176e-05, 1.40062638e-07, -4.16282303e-10)
S_POLY = (5.23598776e-01, -2.39245957e-02, 3.27952196e-04, -2.14001963e-06, 7.95044038e-09)
COS1 = 0.8660254037844386


def horner(coefs, x):
    total = coefs[-1]
    for c in coefs[-2::-1]:
        total = total * x + c
    return total


def lane_index(rows):
    return lax.broadcasted_iota(jnp.int32, (rows, HALF), 1)


def shifted(a, b, k, lane):
    if k == 0:
        return a, b
    zero = jnp.zeros_like(a)
    if k > 0:
        ra = pltpu.roll(a, HALF - k, 1)
        rb = pltpu.roll(b, HALF - k, 1)
        keep = lane < HALF - k
        return jnp.where(keep, ra, rb), jnp.where(keep, rb, zero)
    ra = pltpu.roll(a, -k, 1)
    rb = pltpu.roll(b, -k, 1)
    keep = lane >= -k
    return jnp.where(keep, ra, zero), jnp.where(keep, rb, ra)


def tap_weights(s):
    x = s * s
    f = horner(F_POLY, x)
    c = horner(C_POLY, x)
    q = horner(S_POLY, x)
    sn = s * q
    ss = x * q
    sc = s * c
    n1, n4, n9, n16, n25 = 1.0 - x, 4.0 - x, 9.0 - x, 16.0 - x, 25.0 - x
    h = s * f
    d = n1 * n4
    e = n9 * n16
    k2 = n25 * h
    k3 = e * k2
    k4 = d * k2
    facs = (n4 * k3, -(n1 * k3), n16 * k4, -(n9 * k4), (d * e) * h)
    w0 = ((d * e) * (n25 * f)) * (1.0 + c)
    u1, v1, v2 = COS1 * c, 0.5 * ss, COS1 * ss
    y1, y2, z1, z2 = COS1 * sc, 0.5 * sc, 0.5 * sn, COS1 * sn
    firsts = (1.0 + u1 + v1, 2.0 + c + v2, 3.0 + ss, 4.0 - 2.0 * c + v2, 5.0 - 5.0 * u1 + v1)
    seconds = (s + y1 + z1, s + y2 + 2.0 * z2, s + 3.0 * sn, s - y2 + 4.0 * z2, s - y1 + 5.0 * z1)
    return w0, facs, firsts, seconds


def warp_block(ga, gb, sa, sb, lane):
    outs = []
    pairs = [(shifted(ga, gb, j, lane), shifted(ga, gb, -j, lane)) for j in range(1, TAPS + 1)]
    for half, (g, s) in enumerate(((ga, sa), (gb, sb))):
        w0, facs, firsts, seconds = tap_weights(s)
        total = w0 * g
        for j in range(1, TAPS + 1):
            plus = pairs[j - 1][0][half]
            minus = pairs[j - 1][1][half]
            if j == TAPS:
                plus = jnp.where(s > -1.0, plus, 0.0)
                minus = jnp.where(s < 1.0, minus, 0.0)
            f, t = firsts[j - 1], seconds[j - 1]
            total = total + facs[j - 1] * (f * (plus - minus) + t * (plus + minus))
        outs.append(total)
    return outs


def halves(ref, rows):
    return ref[rows, 0:HALF], ref[rows, HALF:NT]


def first_kernel(g_hbm, s_hbm, gs_ref, left_ref, right_ref, w_ref, part_ref,
                 g_in, s_in, wide_ga, wide_gb, wide_sa, wide_sb, g_sem, s_sem):
    noff, nrow, ncol = 4, 8, 16
    n = nrow * ncol

    def copies(o):
        return (pltpu.make_async_copy(g_hbm.at[o], g_in.at[o], g_sem.at[o]),
                pltpu.make_async_copy(s_hbm.at[o], s_in.at[o], s_sem.at[o]))

    for o in range(noff):
        for c in copies(o):
            c.start()
    lane = lane_index(16)
    side = SIDE * 8

    for o in range(noff):
        for c in copies(o):
            c.wait()
        g = g_in[o].astype(jnp.float32)
        wide_ga[...] = g[:, 0:HALF]
        wide_gb[...] = g[:, HALF:NT]
        wide_sa[...] = s_in[o, :, 0:HALF]
        wide_sb[...] = s_in[o, :, HALF:NT]

        def body(i, _):
            for q in range(2):
                cp = 2 * i + q
                parts = []
                for src in (wide_ga, wide_gb, wide_sa, wide_sb):
                    tiles = [src[pl.ds(2 * cp + k, nrow, stride=ncol), :] for k in range(2)]
                    parts.append(jnp.concatenate(tiles, axis=0))
                ga, gb, sa, sb = parts
                row = pl.ds(pl.multiple_of(o * n + cp * 16, 16), 16)
                gs_ref[0, row, 0:HALF] = ga
                gs_ref[0, row, HALF:NT] = gb
                gs_ref[1, row, 0:HALF] = sa
                gs_ref[1, row, HALF:NT] = sb
                wa, wb = warp_block(ga, gb, sa, sb, lane)
                w_ref[row, 0:HALF] = wa.astype(jnp.bfloat16)
                w_ref[row, HALF:NT] = wb.astype(jnp.bfloat16)
                prow = pl.ds(pl.multiple_of(cp * 16, 16), 16)
                if o == 0:
                    part_ref[prow, 0:HALF] = wa
                    part_ref[prow, HALF:NT] = wb
                else:
                    part_ref[prow, 0:HALF] += wa
                    part_ref[prow, HALF:NT] += wb
            return 0

        lax.fori_loop(0, ncol // 4, body, 0)
        for k in range(2):
            left_ref[k, o * side:(o + 1) * side, :] = gs_ref[k, o * n:o * n + side, :]
            right_ref[k, o * side:(o + 1) * side, :] = gs_ref[k, o * n + n - side:o * n + n, :]


def pack_tile(tiles, row):
    sub = lax.broadcasted_iota(jnp.int32, (8, NT), 0) // 2
    out = None
    for k, t in enumerate(tiles):
        turn = (2 * k - row) % 8
        t = pltpu.roll(t, turn, 0) if turn else t
        out = t if out is None else jnp.where(sub == k, t, out)
    return out


def pack_sides(tiles, odd, depth=0):
    top = pack_tile(tiles, depth)
    bottom = pack_tile(tiles, 6 - depth)
    return jnp.where(odd, bottom, top), jnp.where(odd, top, bottom)


def pack_edges(src, ngroup, odd, send_a, send_b):
    odd = odd != 0

    def body(i, _):
        parts = []
        for j in range(2):
            tiles = [src[pl.ds(pl.multiple_of(i * 64 + 32 * j + 8 * k, 8), 8), :] for k in range(4)]
            parts.append(pack_sides(tiles, odd))
        r = pl.ds(pl.multiple_of(i * 16, 16), 16)
        send_a[r, :] = jnp.concatenate([parts[0][0], parts[1][0]], axis=0).astype(jnp.bfloat16)
        send_b[r, :] = jnp.concatenate([parts[0][1], parts[1][1]], axis=0).astype(jnp.bfloat16)
        return 0

    lax.fori_loop(0, ngroup // 2, body, 0)


def blur_tiles(src, base, slots, dst):
    sub = lax.broadcasted_iota(jnp.int32, (8, NT), 0)
    for k, (below, above, slot) in enumerate(slots):
        r = pl.ds(pl.multiple_of(base + 8 * k, 8), 8)
        cur = src[r, :]
        dn = pltpu.roll(below, 8 - 2 * slot, 0) if slot else below
        up = pltpu.roll(above, 6 - 2 * slot, 0) if slot != 3 else above
        h = jnp.where(sub < 4, dn, up)
        p1 = pltpu.roll(jnp.where(sub >= 1, cur, h), 7, 0)
        p2 = pltpu.roll(jnp.where(sub >= 2, cur, h), 6, 0)
        m1 = pltpu.roll(jnp.where(sub <= 6, cur, h), 1, 0)
        m2 = pltpu.roll(jnp.where(sub <= 5, cur, h), 2, 0)
        dst[r, :] = BINOMIAL[2] * cur + BINOMIAL[1] * (p1 + m1) + BINOMIAL[0] * (p2 + m2)


def blur_rows(src, ngroup, odd, recv_a, recv_b, dst):
    odd = odd != 0

    def body(i, _):
        r = pl.ds(pl.multiple_of(i * 16, 16), 16)
        ra = recv_a[r, :].astype(jnp.float32)
        rb = recv_b[r, :].astype(jnp.float32)
        below = jnp.where(odd, ra, rb)
        above = jnp.where(odd, rb, ra)
        for j in range(2):
            part = slice(8 * j, 8 * j + 8)
            blur_tiles(src, i * 64 + 32 * j, [(below[part], above[part], k) for k in range(4)], dst)
        return 0

    lax.fori_loop(0, ngroup // 2, body, 0)


def blur_rows_own(u_ref, odd, dst):
    odd = odd != 0
    wide = 16 + 2 * SIDE
    per = wide // 4
    sides = 4 * wide * 8

    def body(i, _):
        o = lax.div(i, per)
        q = lax.rem(i, per)
        pairs = []
        for t in range(2):
            row = sides + o * 64 + (q + t) * 8
            ra = u_ref[pl.ds(pl.multiple_of(row, 8), 8), :]
            rb = u_ref[pl.ds(pl.multiple_of(row + 256, 8), 8), :]
            pairs.append((jnp.where(odd, ra, rb), jnp.where(odd, rb, ra)))
        slots = [(*pairs[(k + 2) // 4], (k + 2) % 4) for k in range(4)]
        blur_tiles(u_ref, i * 32, slots, dst)
        return 0

    lax.fori_loop(0, 4 * per, body, 0)


def blur_cols(src, start, rows):
    total = None
    for k, w in enumerate(BINOMIAL):
        v = src[pl.ds(pl.multiple_of(start + 8 * k, 8), rows), :]
        total = w * v if total is None else total + w * v
    return total


def split(v):
    high = v.astype(jnp.bfloat16)
    return high, (v - high.astype(jnp.float32)).astype(jnp.bfloat16)


def joined(ref, row, count):
    return ref[row:row + count, :].astype(jnp.float32) + ref[row + count:row + 2 * count, :].astype(jnp.float32)


def stack_kernel(odd_ref, mine_ref, other_ref, w_ref, stack_ref, a_ref, b_ref, *, scale):
    odd = odd_ref[0] != 0
    stack_ref[...] = (mine_ref[...] + other_ref[...].astype(jnp.float32)) * scale

    def warped(i, _):
        parts = []
        for j in range(2):
            w = w_ref[pl.ds(pl.multiple_of(i * 64 + 32 * j, 32), 32), :].astype(jnp.float32)
            parts.append(pack_sides([w[8 * k:8 * k + 8] for k in range(4)], odd))
        r = pl.ds(pl.multiple_of(i * 16, 16), 16)
        a_ref[r, :] = jnp.concatenate([parts[0][0], parts[1][0]], axis=0).astype(jnp.bfloat16)
        b_ref[r, :] = jnp.concatenate([parts[0][1], parts[1][1]], axis=0).astype(jnp.bfloat16)
        return 0

    lax.fori_loop(0, 8, warped, 0)
    for depth in (0, 2):
        parts = [pack_sides([stack_ref[32 * q + 8 * k:32 * q + 8 * k + 8, :] for k in range(4)], odd, depth)
                 for q in range(4)]
        for ref, side in ((a_ref, 0), (b_ref, 1)):
            high, low = split(jnp.concatenate([p[side] for p in parts], axis=0))
            row = 128 + 32 * depth
            ref[row:row + 32, :] = high
            ref[row + 32:row + 64, :] = low


def stack_blur_kernel(odd_ref, stack_ref, a_ref, b_ref, v_ref, va_ref, vb_ref, left_ref, right_ref):
    odd = odd_ref[0] != 0
    sub = lax.broadcasted_iota(jnp.int32, (32, NT), 0)
    even_row = lax.rem(sub, 2) == 0

    def exchanged(x):
        return jnp.where(even_row, pltpu.roll(x, 31, 0), pltpu.roll(x, 1, 0))

    tiles = [[stack_ref[32 * q + 8 * k:32 * q + 8 * k + 8, :] for k in range(4)] for q in range(4)]
    own = [pack_sides(t, odd) for t in tiles]
    first_a, second_a = joined(a_ref, 128, 32), joined(a_ref, 192, 32)
    first_b, second_b = joined(b_ref, 128, 32), joined(b_ref, 192, 32)
    below = jnp.where(odd, first_a, first_b)
    above = jnp.where(odd, first_b, first_a)
    for q in range(4):
        part = slice(8 * q, 8 * q + 8)
        blur_tiles(stack_ref, 32 * q, [(below[part], above[part], k) for k in range(4)], v_ref)
    even = jnp.where(even_row, 1.0, 0.0)
    flag = jnp.where(odd, 1.0, 0.0)
    for ref, side, near, far, down in ((va_ref, 0, first_a, second_a, flag), (vb_ref, 1, first_b, second_b, 1.0 - flag)):
        edge = jnp.concatenate([p[side] for p in own], axis=0)
        inner = jnp.where(even == down, exchanged(edge), exchanged(far))
        ref[...] = (BINOMIAL[2] * near + BINOMIAL[1] * (exchanged(near) + inner) + BINOMIAL[0] * (edge + far))
    for ref, c in ((left_ref, 0), (right_ref, 1)):
        high, low = split(v_ref[64 * c:64 * c + 64, :])
        ref[0:64, :] = high
        ref[64:128, :] = low
        for k, (v, w) in enumerate(((va_ref, a_ref), (vb_ref, b_ref))):
            high, low = split(v[16 * c:16 * c + 16, :])
            row = 128 + 96 * k
            ref[row:row + 16, :] = high
            ref[row + 16:row + 32, :] = low
            for o in range(4):
                ref[row + 32 + 16 * o:row + 48 + 16 * o, :] = w[32 * o + 16 * c:32 * o + 16 * c + 16, :]


SCALE = GAIN * 1.4426950408889634
GROUP = 32


def store_products(wa, wb, pa, pb, first, buf_a, buf_b, lane):
    block = buf_a.shape[0] // (2 * NLAG)
    ea, eb = wa * wa, wb * wb
    for l in range(NLAG):
        va, vb = shifted(wa, wb, l - LAGS, lane)
        r = l * block + first
        buf_a[r:r + 16, :] = pa * va
        buf_b[r:r + 16, :] = pb * vb
        va, vb = shifted(ea, eb, l - LAGS, lane)
        r += NLAG * block
        buf_a[r:r + 16, :] = va
        buf_b[r:r + 16, :] = vb


def finish_update(buf_a, buf_b, smooth_ref, pe_ref, pe_rows, u_ref, u_row):
    block = buf_a.shape[0] // (2 * NLAG)
    rows = jnp.concatenate([buf_a[...], buf_b[...]], axis=1)
    sums = jnp.dot(rows, smooth_ref[...], preferred_element_type=jnp.float32)
    for first in range(0, block, 16):
        pe_row = pl.multiple_of(pe_rows[first // GROUP] + first % GROUP, 16)
        for lo in (0, HALF):
            pe = pe_ref[pl.ds(pe_row, 16), lo:lo + HALF]
            scores = []
            for l in range(NLAG):
                r = l * block + first
                co = sums[r:r + 16, lo:lo + HALF]
                r += NLAG * block
                le = sums[r:r + 16, lo:lo + HALF]
                scores.append(jnp.exp2(co * lax.rsqrt(pe * le + EPS / SCALE**2)))
            den = scores[LAGS]
            run = num = None
            for k in range(LAGS, 0, -1):
                up, down = scores[LAGS + k], scores[LAGS - k]
                den = den + (up + down)
                run = up - down if run is None else run + (up - down)
                num = run if num is None else num + run
            u_ref[pl.ds(pl.multiple_of(u_row + first, 16), 16), lo:lo + HALF] = num / den


def pipeline(count, many, place, prepare, finish):
    def places(i):
        return [place(i * many + k) for k in range(many)]

    prepare(places(0))

    def body(i, _):
        finish(i - 1, places(i - 1))
        prepare(places(i))
        return 0

    lax.fori_loop(1, count // many, body, 0)
    finish(count // many - 1, places(count // many - 1))


def halo_kernel(gs_ref, w_ref, hl_ref, hr_ref, g_out, s_out, w_out):
    ncol = 16 + 2 * SIDE
    lane = lane_index(16)
    side = SIDE * 8
    for o in range(4):
        n = o * ncol * 8
        m = o * 128
        g_out[n + side:n + side + 128, :] = gs_ref[0, m:m + 128, :]
        s_out[n + side:n + side + 128, :] = gs_ref[1, m:m + 128, :]
        w_out[n + side:n + side + 128, :] = w_ref[m:m + 128, :]

    def body(i, _):
        o = i // (SIDE // 2)
        hp = lax.rem(i, SIDE // 2)
        src = pl.ds(pl.multiple_of(i * 16, 16), 16)
        for ref, first in ((hl_ref, 0), (hr_ref, ncol - SIDE)):
            dst = pl.ds(pl.multiple_of(o * ncol * 8 + first * 8 + hp * 16, 16), 16)
            ga, gb = ref[0, src, 0:HALF], ref[0, src, HALF:NT]
            sa, sb = ref[1, src, 0:HALF], ref[1, src, HALF:NT]
            g_out[dst, 0:HALF] = ga
            g_out[dst, HALF:NT] = gb
            s_out[dst, 0:HALF] = sa
            s_out[dst, HALF:NT] = sb
            wa, wb = warp_block(ga, gb, sa, sb, lane)
            w_out[dst, 0:HALF] = wa.astype(jnp.bfloat16)
            w_out[dst, HALF:NT] = wb.astype(jnp.bfloat16)
        return 0

    lax.fori_loop(0, 4 * SIDE // 2, body, 0)


def pilot_kernel(v_ref, va_ref, vb_ref, a_ref, b_ref, sl_ref, sr_ref, w_ref, smooth_ref,
                 pilot_ref, pe_ref, u_ref, vext, vside, w_all, buf_a, buf_b):
    ncol = 16 + 2 * SIDE
    main = 4 * ncol * 8
    own = ncol * 8
    vext[0:64, :] = joined(sl_ref, 0, 64)
    vext[64:192, :] = v_ref[...]
    vext[192:256, :] = joined(sr_ref, 0, 64)
    w_all[0:main, :] = w_ref[...]
    pad = jnp.zeros((8, NT), jnp.float32)
    for k, (v, w) in enumerate(((va_ref, a_ref), (vb_ref, b_ref))):
        row = 128 + 96 * k
        vside[k, 0:8, :] = pad
        vside[k, 72:80, :] = pad
        vside[k, 8:24, :] = joined(sl_ref, row, 16)
        vside[k, 24:56, :] = v[...]
        vside[k, 56:72, :] = joined(sr_ref, row, 16)
        for o in range(4):
            base = main + 256 * k + 64 * o
            src = slice(row + 32 + 16 * o, row + 48 + 16 * o)
            w_all[base:base + 16, :] = sl_ref[src, :]
            w_all[base + 16:base + 48, :] = w[32 * o:32 * o + 32, :]
            w_all[base + 48:base + 64, :] = sr_ref[src, :]
        total = None
        for t, weight in enumerate(BINOMIAL):
            piece = vside[k, 4 + 2 * t:68 + 2 * t, :]
            total = weight * piece if total is None else total + weight * piece
        pilot_ref[own + 64 * k:own + 64 * k + 64, :] = total.astype(jnp.bfloat16)

    def make_pilot(i, _):
        r = pl.ds(pl.multiple_of(i * 16, 16), 16)
        pilot_ref[r, :] = blur_cols(vext, i * 16, 16).astype(jnp.bfloat16)
        return 0

    lax.fori_loop(0, ncol // 2, make_pilot, 0)
    sq = jnp.square(pilot_ref[...].astype(jnp.float32)).astype(jnp.bfloat16)
    pe_ref[...] = jnp.dot(sq, smooth_ref[...], preferred_element_type=jnp.float32) * (1.0 / SCALE**2)

    lane = lane_index(16)
    per = ncol * 8 // GROUP

    def place(g):
        h = g - 4 * per
        side = own + 64 * lax.div(h, 8) + GROUP * lax.rem(h, 2)
        return g, jnp.where(g < 4 * per, GROUP * lax.rem(g, per), side)

    def prepare(places):
        for first in range(0, len(places) * GROUP, 16):
            g, prow = places[first // GROUP]
            wr = pl.ds(pl.multiple_of(g * GROUP + first % GROUP, 16), 16)
            pr = pl.ds(pl.multiple_of(prow + first % GROUP, 16), 16)
            wa, wb = halves(w_all, wr)
            pa, pb = halves(pilot_ref, pr)
            store_products(wa, wb, pa, pb, first, buf_a, buf_b, lane)

    def finish(j, places):
        finish_update(buf_a, buf_b, smooth_ref, pe_ref, [p for _, p in places], u_ref, j * len(places) * GROUP)

    pipeline(4 * per + 16, 2, place, prepare, finish)


def step_kernel(odd_ref, u_old, *refs, ncol, local):
    if not local:
        ra_ref, rb_ref, *refs = refs
    s_old, g_ref, pilot_ref, pe_ref, smooth_ref, s_out, u_ref, a_ref, b_ref, vbuf, buf_a, buf_b = refs
    wide = ncol + 4
    skip = (16 + 2 * SIDE - ncol) // 2
    if local:
        blur_rows_own(u_old, odd_ref[0], vbuf)
    else:
        blur_rows(u_old, wide, odd_ref[0], ra_ref, rb_ref, vbuf)
    lane = lane_index(16)
    per = ncol * 8 // GROUP

    def place(g):
        return lax.div(g, per), lax.rem(g, per)

    def prepare(places):
        for first in range(0, len(places) * GROUP, 16):
            o, q = places[first // GROUP]
            row = q * GROUP + first % GROUP
            src = o * wide * 8 + row
            dst = pl.ds(pl.multiple_of(o * ncol * 8 + row, 16), 16)
            sr = pl.ds(pl.multiple_of(src + 16, 16), 16)
            gr = pl.ds(pl.multiple_of(o * (16 + 2 * SIDE) * 8 + skip * 8 + row, 16), 16)
            pr = pl.ds(pl.multiple_of(skip * 8 + row, 16), 16)
            s = LIMIT * jnp.tanh((s_old[sr, :] + blur_cols(vbuf, src, 16)) / LIMIT)
            s_out[dst, :] = s
            ga, gb = halves(g_ref, gr)
            wa, wb = warp_block(ga, gb, s[:, 0:HALF], s[:, HALF:NT], lane)
            pa, pb = halves(pilot_ref, pr)
            store_products(wa.astype(jnp.bfloat16), wb.astype(jnp.bfloat16), pa, pb, first, buf_a, buf_b, lane)

    def finish(j, places):
        rows = [skip * 8 + q * GROUP for _, q in places]
        finish_update(buf_a, buf_b, smooth_ref, pe_ref, rows, u_ref, j * len(places) * GROUP)

    pipeline(4 * per, 1, place, prepare, finish)
    pack_edges(u_ref, ncol, odd_ref[0], a_ref, b_ref)


def last_kernel(odd_ref, u_old, ra_ref, rb_ref, s_old, out_hbm, vbuf, out_a, out_b, out, sem):
    wide = 16 + 4
    blur_rows(u_old, wide, odd_ref[0], ra_ref, rb_ref, vbuf)

    def copy(o):
        return pltpu.make_async_copy(out.at[o], out_hbm.at[o], sem.at[o])

    def body(o, _):
        for cp in range(8):
            src = pl.multiple_of(o * wide * 8 + cp * 16, 16)
            sr = pl.ds(pl.multiple_of(o * wide * 8 + 16 + cp * 16, 16), 16)
            s = LIMIT * jnp.tanh((s_old[sr, :] + blur_cols(vbuf, src, 16)) / LIMIT)
            for k in range(2):
                r = pl.ds(2 * cp + k, 8, stride=16)
                out_a[r, :] = s[8 * k:8 * k + 8, 0:HALF]
                out_b[r, :] = s[8 * k:8 * k + 8, HALF:NT]
        out[o, :, 0:HALF] = out_a[...]
        out[o, :, HALF:NT] = out_b[...]
        copy(o).start()
        return 0

    lax.fori_loop(0, 4, body, 0)
    for o in range(4):
        copy(o).wait()


VMEM = pl.BlockSpec(memory_space=pltpu.VMEM)
SMEM = pl.BlockSpec(memory_space=pltpu.SMEM)
HBM = pl.BlockSpec(memory_space=pltpu.HBM)
DMA = pltpu.SemaphoreType.DMA
F32 = jnp.float32
BF16 = jnp.bfloat16


def call(kernel, args, outs, scratch=(), ins=None, out_specs=None, flops=10**8, name=None):
    return pl.pallas_call(
        kernel,
        out_shape=[jax.ShapeDtypeStruct(s, d) for s, d in outs],
        in_specs=ins or [SMEM] + [VMEM] * (len(args) - 1),
        out_specs=out_specs or [VMEM] * len(outs),
        scratch_shapes=[pltpu.VMEM(*s) if isinstance(s, tuple) else s for s in scratch],
        compiler_params=pltpu.CompilerParams(vmem_limit_bytes=16 * 2**20),
        cost_estimate=pl.CostEstimate(flops=flops, bytes_accessed=2 * 10**6, transcendentals=0),
        name=name,
    )(*args)


def swap(cells, axis, first):
    count = lax.axis_size(axis)
    pairs = []
    for i in range(first, count - 1, 2):
        pairs += [(i, i + 1), (i + 1, i)]
    return lax.ppermute(cells, axis, pairs)


def ship(cells, axis, step):
    count = lax.axis_size(axis)
    return lax.ppermute(cells, axis, [(i, i + step) for i in range(count) if 0 <= i + step < count])


def smoother():
    d = jnp.abs(jnp.arange(NT)[:, None] - jnp.arange(NT)[None, :]).astype(F32)
    return (jnp.maximum(RAMP - d, 0.0) / RAMP).astype(BF16)


def shards(gathers, shift_start):
    odd = lax.rem(lax.axis_index("inl"), 2).astype(jnp.int32).reshape(1)
    smooth = smoother()
    rows = 4 * 8 * 16
    side = 4 * SIDE * 8
    gs, to_left, to_right, w_own, part = call(
        first_kernel,
        [gathers.reshape(4, 128, NT), shift_start.reshape(4, 128, NT)],
        [((2, rows, NT), F32), ((2, side, NT), F32), ((2, side, NT), F32), ((rows, NT), BF16), ((128, NT), F32)],
        [((4, 128, NT), BF16), ((4, 128, NT), F32)] + [((128, HALF), F32)] * 4 + [DMA((4,)), DMA((4,))],
        ins=[HBM, HBM], name="first",
    )
    part = part + lax.ppermute(part, "off", [(i, i ^ 1) for i in range(8)])
    part = part + lax.ppermute(part.astype(BF16), "off", [(i, i ^ 2) for i in range(8)]).astype(F32)
    other = lax.ppermute(part.astype(BF16), "off", [(i, 2 * (3 - i // 2) + i % 2) for i in range(8)])
    halo_left = ship(to_right, "xl", 1)
    halo_right = ship(to_left, "xl", -1)
    total = 4 * lax.axis_size("off")
    stack, a, b = call(
        functools.partial(stack_kernel, scale=1.0 / total), [odd, part, other, w_own],
        [((128, NT), F32), ((256, NT), BF16), ((256, NT), BF16)], name="stack",
    )
    ra, rb = swap(a, "inl", 1), swap(b, "inl", 0)
    v, va, vb, ship_left, ship_right = call(
        stack_blur_kernel, [odd, stack, ra, rb],
        [((128, NT), F32), ((32, NT), F32), ((32, NT), F32), ((320, NT), BF16), ((320, NT), BF16)], name="stackblur",
    )
    sl = ship(ship_right, "xl", 1)
    sr = ship(ship_left, "xl", -1)

    ncol = 16 + 2 * SIDE
    n = 4 * ncol * 8
    g_ext, s_ext, w_ext = call(
        halo_kernel, [gs, w_own, halo_left, halo_right],
        [((n, NT), F32), ((n, NT), F32), ((n, NT), BF16)], ins=[VMEM] * 4, name="halo",
    )

    def work(block):
        return [((2 * NLAG * block, HALF), BF16)] * 2

    pilot, pe, u = call(
        pilot_kernel, [v, va, vb, ra, rb, sl, sr, w_ext, smooth],
        [((ncol * 8 + 128, NT), BF16), ((ncol * 8 + 128, NT), F32), ((n + 512, NT), F32)],
        [((256, NT), F32), ((2, 80, NT), F32), ((n + 512, NT), BF16)] + work(64), ins=[VMEM] * 9, name="pilot",
    )
    for it in range(ITERS - 1):
        near = [swap(a, "inl", 1), swap(b, "inl", 0)] if it else []
        ncol -= 4
        n = 4 * ncol * 8
        s_ext, u, a, b = call(
            functools.partial(step_kernel, ncol=ncol, local=it == 0),
            [odd, u, *near, s_ext, g_ext, pilot, pe, smooth],
            [((n, NT), F32), ((n, NT), F32), ((n // 4, NT), BF16), ((n // 4, NT), BF16)],
            [((4 * (ncol + 4) * 8, NT), F32)] + work(32), name="step%d" % ncol,
        )
    ra, rb = swap(a, "inl", 1), swap(b, "inl", 0)
    (out,) = call(
        last_kernel, [odd, u, ra, rb, s_ext], [((4, 128, NT), F32)],
        [((n, NT), F32), ((128, HALF), F32), ((128, HALF), F32), ((4, 128, NT), F32), DMA((4,))],
        out_specs=[HBM], name="last",
    )
    return out.reshape(shift_start.shape)


def solution(mesh):
    spec = P("off", "inl", "xl", None)
    return jax.shard_map(shards, mesh=mesh, in_specs=(spec, spec), out_specs=spec, check_vma=False)
```
